32 devices in a mesh: dp: 8 (over y, x, core), seq: 4 (over z).
Axes of the slice: x: 2, y: 2, z: 4, core: 2. Of those that a mesh axis runs over, the one named last changes fastest.
Arguments:
- queries: bfloat16 [4096, 4096], P(('dp', 'seq')), may hold values from -300 to 300
- key_proj: bfloat16 [4096, 512], P(('dp', 'seq')), may hold values from -4.5 to 4.5
- value_proj: bfloat16 [4096, 512], P(('dp', 'seq')), may hold values from -6 to 6
- seq_lengths: int32 [32], replicated, may hold values from 1 to 257, 4096 in all
Outputs:
- attended: bfloat16 [4096, 4096], P(('dp', 'seq'))
The draws below stay inside these ranges and needn't reach their ends.
Inputs may be any that keep to these rules, and one draw needn't show every extreme that they name: `seq_lengths`: the sequences cover all 4096 tokens; the longest has exactly 257 tokens.
All inputs are finite; a program needn't handle non-finite values.
Results may differ from the reference program's by a relative error of at most 0.0036.
Values may be sent and summed in bfloat16 or wider, within the bound.
No kernel may reach another device: no remote copies, remote signals or barrier semaphores. Data moves between devices by JAX's collectives and lax.ppermute only.
A program may use at most 64 MiB of HBM per device.

```python
import math
import jax
import jax.numpy as jnp
import numpy as np
from jax import lax

HD = 128
QH = 32
KVH = 4
BLOCK = 512
REACH = 256
TOKENS = 4096
COUNT = 32


def normal_keys(key):
    return jax.random.truncated_normal(jax.random.fold_in(key, 11), -4.5, 4.5, (TOKENS, KVH * HD), jnp.float32)


def draw_key_proj(key, part):
    return normal_keys(key).astype(jnp.bfloat16)


def draw_queries(key, part):
    drawn = jax.random.truncated_normal(jax.random.fold_in(key, 12), -4.5, 4.5, (TOKENS, QH * HD), jnp.float32)
    return drawn.astype(jnp.bfloat16)


def block_scale(own_key, dims, split, smallest, top_value):
    def one(axis_at, shards_of):
        heights = jax.random.uniform(jax.random.fold_in(jax.random.fold_in(own_key, 6), axis_at), (shards_of,), jnp.float32, smallest / len(split), top_value / len(split))
        return jnp.repeat(jnp.exp(heights), dims[axis_at] // shards_of).reshape((-1,) + (1,) * (len(dims) - axis_at - 1))

    loudness = one(*split[0])
    for cut in split[1:]:
        loudness = loudness * one(*cut)
    return loudness


def profile(count, total, most, slope):
    portions = [(1 << 20) // math.isqrt(standing ** slope) + 1 for standing in range(2, count + 1)]
    rest, counts = total - most - (count - 1), [1] * (count - 1)
    while rest > 0:
        free = [i for i in range(count - 1) if counts[i] < most]
        mass, left = sum([portions[i] for i in free]), rest
        for i in free:
            extra = min(most - counts[i], max(1, left * portions[i] // mass), rest)
            counts[i] = counts[i] + extra
            rest = rest - extra
    return np.array([most] + counts)


def ragged_sizes(key, count, total, most, slope):
    if count == 2:
        one = jax.random.randint(key, (), max(1, total - most), min(most, total - 1) + 1)
        return jnp.stack([one, total - one])
    lengths = jnp.asarray(profile(count, total, most, slope), jnp.int32)
    twos = (count - 1) // 2
    giver, receiver = lengths[1:1 + 2 * twos:2], lengths[2:2 + 2 * twos:2]
    slack = jnp.minimum(giver - 1, most - receiver)
    passed = jax.random.randint(jax.random.fold_in(key, 1), (twos,), 0, 1 << 20) % (slack + 1)
    lengths = lengths.at[1:1 + 2 * twos:2].set(giver - passed).at[2:2 + 2 * twos:2].set(receiver + passed)
    return lengths[jax.random.permutation(jax.random.fold_in(key, 2), count)]


def gaussian(key, extent, scale, limit, split=(), held_as=jnp.bfloat16):
    result = jax.random.normal(key, extent, jnp.float32) * scale
    if len(split) > 0:
        result = block_scale(key, extent, split, -0.22, 0.18) * result
    return jnp.clip(result, min=-limit, max=limit).astype(held_as)


def setup_inputs(seed: int = 0) -> dict:
    keys = jax.random.split(jax.random.key(seed), 5)
    queries = draw_queries(jax.random.fold_in(keys[4], 71), 0)
    key_proj = draw_key_proj(jax.random.fold_in(keys[4], 71), 0)
    value_proj = gaussian(keys[2], (TOKENS, KVH * HD), 1.0, 6.0, ((0, 32),))
    seq_lengths = ragged_sizes(keys[3], COUNT, TOKENS, REACH + 1, 1).astype(jnp.int32)
    return {"queries": queries, "key_proj": key_proj, "value_proj": value_proj, "seq_lengths": seq_lengths}


score_scale = 0.08838834764831845
neg_fill = -1e30


def reference(queries, key_proj, value_proj, seq_lengths):
    tile_rows = math.gcd(BLOCK, 512)
    group_size = QH // KVH
    query_all = queries.reshape(TOKENS, QH, HD)
    keys_padded = jnp.concatenate([jnp.zeros((REACH, KVH, HD), jnp.bfloat16), key_proj.reshape(TOKENS, KVH, HD)], axis=0)
    values_padded = jnp.concatenate([jnp.zeros((REACH, KVH, HD), jnp.bfloat16), value_proj.reshape(TOKENS, KVH, HD)], axis=0)
    seq_ends = jnp.cumsum(seq_lengths).astype(jnp.int32)
    begins = (seq_ends - seq_lengths).astype(jnp.int32)
    window = tile_rows + REACH

    def one_tile(tile_index):
        offset = (tile_index * tile_rows).astype(jnp.int32)
        query_tile = lax.dynamic_slice_in_dim(query_all, offset, tile_rows, 0).astype(jnp.float32)
        key_window = lax.dynamic_slice_in_dim(keys_padded, offset, window, 0)
        value_window = lax.dynamic_slice_in_dim(values_padded, offset, window, 0)
        query_pos = offset + jnp.arange(tile_rows, dtype=jnp.int32)
        key_pos = offset - REACH + jnp.arange(window, dtype=jnp.int32)
        covered = begins[None, :] <= query_pos[:, None]
        starts = jnp.max(jnp.where(covered, begins[None, :], 0), axis=1).astype(jnp.int32)
        allowed = (key_pos[None, :] <= query_pos[:, None]) & (key_pos[None, :] >= starts[:, None])
        key_heads = jnp.repeat(key_window, group_size, axis=1).astype(jnp.float32)
        value_heads = jnp.repeat(value_window, group_size, axis=1).astype(jnp.float32)
        scores = jnp.einsum('qhd,khd->hqk', query_tile, key_heads) * score_scale
        scores = jnp.where(allowed[None], scores, neg_fill)
        row_max = jnp.max(scores, axis=2, keepdims=True)
        weights = jnp.where(allowed[None], jnp.exp(scores - row_max), 0.0)
        row_sum = jnp.sum(weights, axis=2)
        rounded = lax.optimization_barrier(weights.astype(jnp.bfloat16)).astype(jnp.float32)
        mixed = jnp.einsum('hqk,khd->hqd', rounded, value_heads) / row_sum[..., None]
        return jnp.transpose(mixed, (1, 0, 2)).reshape(tile_rows, QH * HD).astype(jnp.bfloat16)

    pieces = lax.map(one_tile, jnp.arange(TOKENS // tile_rows, dtype=jnp.int32))
    return pieces.reshape(TOKENS, QH * HD)
```

```python
import functools
import math

import jax
import jax.numpy as jnp
from jax import lax
from jax.experimental import pallas as pl
from jax.experimental.pallas import tpu as pltpu
from jax.sharding import PartitionSpec as P

HD = 128

AXES = ("dp", "seq")
score_scale = 0.08838834764831845
neg_fill = -1e30


def from_behind(block, distance):
    count = lax.axis_size(AXES)
    return lax.ppermute(block, AXES, [(i, i + distance) for i in range(count - distance)])


def attend_kernel(chunks, group, lengths_ref, q_ref, *refs):
    key_refs = refs[:chunks]
    value_refs = refs[chunks : 2 * chunks]
    out_ref, bias_ref, value_ref = refs[2 * chunks :]
    rows = q_ref.shape[0]
    span = chunks * rows

    @pl.when(pl.program_id(0) == 0)
    def _():
        first = lax.axis_index(AXES) * rows
        key_pos = lax.broadcasted_iota(jnp.int32, (8, span), 1) + (first - span + rows)

        def step(i, carry):
            end, last = carry
            end = end + lengths_ref[i]
            return end, jnp.where(key_pos < end, jnp.minimum(last, end - 1), last)

        top = jnp.full((8, span), jnp.iinfo(jnp.int32).max, jnp.int32)
        _, last = lax.fori_loop(0, lengths_ref.shape[0], step, (jnp.int32(0), top), unroll=4)
        last = jnp.where(key_pos < 0, -1, last)
        query_pos = lax.broadcasted_iota(jnp.int32, (rows, span), 0) + first
        allowed = (query_pos >= key_pos[:1]) & (query_pos <= last[:1])
        bias_ref[...] = jnp.where(allowed, 0.0, neg_fill)
        value_ref[:, HD:] = jnp.ones((span, HD), value_ref.dtype)

    keys = jnp.concatenate([ref[...] for ref in key_refs], axis=0)
    for i, ref in enumerate(value_refs):
        value_ref[i * rows : (i + 1) * rows, :HD] = ref[...]
    values = value_ref[...]
    bias = bias_ref[...]
    for head in range(group):
        at = slice(head * HD, (head + 1) * HD)
        scores = lax.dot_general(
            q_ref[:, at], keys, (((1,), (1,)), ((), ())), preferred_element_type=jnp.float32
        )
        scores = scores + bias
        row_max = jnp.max(scores, axis=1, keepdims=True)
        weights = jnp.exp2((scores - row_max) * (score_scale * math.log2(math.e)))
        mixed = jnp.dot(weights.astype(jnp.bfloat16), values, preferred_element_type=jnp.float32)
        out_ref[:, at] = (mixed[:, :HD] / mixed[:, HD:]).astype(out_ref.dtype)


def attend(queries, keys, values, seq_lengths):
    rows = queries.shape[0]
    chunks = len(keys)
    shared = keys[0].shape[1] // HD
    group = queries.shape[1] // keys[0].shape[1]
    wide = pl.BlockSpec((rows, group * HD), lambda h: (0, h))
    narrow = pl.BlockSpec((rows, HD), lambda h: (0, h))
    return pl.pallas_call(
        functools.partial(attend_kernel, chunks, group),
        grid=(shared,),
        in_specs=[pl.BlockSpec(memory_space=pltpu.SMEM), wide] + [narrow] * (2 * chunks),
        out_specs=wide,
        out_shape=jax.ShapeDtypeStruct(queries.shape, queries.dtype),
        scratch_shapes=[
            pltpu.VMEM((rows, chunks * rows), jnp.float32),
            pltpu.VMEM((chunks * rows, 2 * HD), jnp.bfloat16),
        ],
        name="attend",
    )(seq_lengths, queries, *keys, *values)


def body(queries, key_proj, value_proj, seq_lengths):
    rows = queries.shape[0]
    reach = rows * lax.axis_size("seq") // 2
    behind = -(-reach // rows)
    keys, values = [key_proj], [value_proj]
    for distance in range(1, behind + 1):
        keys.insert(0, from_behind(key_proj, distance))
        values.insert(0, from_behind(value_proj, distance))
    return attend(queries, keys, values, seq_lengths)


def solution(mesh):
    return jax.shard_map(
        body,
        mesh=mesh,
        in_specs=(P(AXES, None), P(AXES, None), P(AXES, None), P()),
        out_specs=P(AXES, None),
        check_vma=False,
    )
```

```python
import functools
import math

import jax
import jax.numpy as jnp
from jax import lax
from jax.experimental import pallas as pl
from jax.experimental.pallas import tpu as pltpu
from jax.sharding import PartitionSpec as P

HD = 128
STACK = 4
VMEM_LIMIT = 24 << 20

AXES = ("dp", "seq")
score_scale = 0.08838834764831845
neg_fill = -1e30
exp2_scale = score_scale * math.log2(math.e)

F32 = jnp.float32
BF16 = jnp.bfloat16


def shift(block, distance, keep=lambda target: True):
    count = lax.axis_size(AXES)
    return lax.ppermute(
        block, AXES, [(t - distance, t) for t in range(distance, count) if keep(t)]
    )


def head(index, count=1):
    return slice(index * HD, (index + count) * HD)


def row_stack(ref, columns):
    return jnp.concatenate([ref[:, at] for at in columns], axis=0)


def mask_bias(lengths_ref, rows, span):
    first = lax.axis_index(AXES) * rows
    key_pos = lax.broadcasted_iota(jnp.int32, (8, span), 1) + (first - span + rows)

    def step(i, carry):
        end, last = carry
        end = end + lengths_ref[i]
        return end, jnp.where(key_pos < end, jnp.minimum(last, end - 1), last)

    top = jnp.full((8, span), jnp.iinfo(jnp.int32).max, jnp.int32)
    _, last = lax.fori_loop(0, lengths_ref.shape[0], step, (jnp.int32(0), top), unroll=4)
    last = jnp.where(key_pos < 0, -1, last)
    query_pos = lax.broadcasted_iota(jnp.int32, (rows, span), 0) + first
    allowed = (query_pos >= key_pos[:1]) & (query_pos <= last[:1])
    return jnp.where(allowed, 0.0, neg_fill)


def near_kernel(chunks, group, lengths_ref, q_ref, *refs):
    key_refs = refs[:chunks]
    value_refs = refs[chunks : 2 * chunks]
    max_ref, sum_ref, mixed_ref, far_bias_ref, value_ref = refs[2 * chunks :]
    rows = q_ref.shape[0]
    span = chunks * rows
    shared = key_refs[0].shape[1] // HD
    bias = mask_bias(lengths_ref, rows, span + rows)
    far_bias_ref[...] = bias[:, :rows]
    bias = jnp.concatenate([bias[:, rows:]] * STACK, axis=0)
    value_ref[:, HD:] = jnp.ones((span, HD), value_ref.dtype)
    for kv in range(shared):
        keys = jnp.concatenate([ref[:, head(kv)] for ref in key_refs], axis=0)
        for i, ref in enumerate(value_refs):
            value_ref[i * rows : (i + 1) * rows, :HD] = ref[:, head(kv)]
        values = value_ref[...]
        for first in range(kv * group, (kv + 1) * group, STACK):
            columns = [head(first + i) for i in range(STACK)]
            scores = lax.dot_general(
                row_stack(q_ref, columns),
                keys,
                (((1,), (1,)), ((), ())),
                preferred_element_type=F32,
            )
            scores = scores + bias
            row_max = jnp.max(scores, axis=1, keepdims=True)
            weights = jnp.exp2((scores - row_max) * exp2_scale).astype(BF16)
            mixed = jnp.dot(weights, values, preferred_element_type=F32)
            row_max = jnp.broadcast_to(row_max, (STACK * rows, HD))
            for i, at in enumerate(columns):
                part = slice(i * rows, (i + 1) * rows)
                max_ref[:, at] = row_max[part]
                mixed_ref[:, at] = mixed[part, :HD]
                sum_ref[:, at] = mixed[part, HD:]


def block_diagonal(ref, a, b, scratch):
    rows = ref.shape[0]
    scratch[:rows, :HD] = ref[:, head(a)]
    scratch[rows:, HD:] = ref[:, head(b)]
    scratch[:rows, HD:] = jnp.zeros((rows, HD), scratch.dtype)
    scratch[rows:, :HD] = jnp.zeros((rows, HD), scratch.dtype)
    return scratch[...]


def far_kernel(group, q_ref, key_ref, value_ref, relay_ref, bias_ref, max_ref, sum_ref, mixed_ref, out_ref,
               far_value_ref, pair_keys, pair_values, staged_ref, sems):
    rows = q_ref.shape[0]
    shared = key_ref.shape[1] // HD
    far_value_ref[...] = value_ref[...] + relay_ref[...]
    bias = jnp.concatenate([bias_ref[...]] * STACK, axis=0)
    bias = jnp.concatenate([bias] * 2, axis=1)
    copies = []
    for a in range(0, shared, 2):
        b = a + 1
        keys = block_diagonal(key_ref, a, b, pair_keys)
        values = block_diagonal(far_value_ref, a, b, pair_values)
        for first in range(0, group, STACK):
            left = [head(a * group + first + i) for i in range(STACK)]
            right = [head(b * group + first + i) for i in range(STACK)]

            def both(ref):
                return jnp.concatenate([row_stack(ref, left), row_stack(ref, right)], axis=1)

            scores = lax.dot_general(
                both(q_ref), keys, (((1,), (1,)), ((), ())), preferred_element_type=F32
            )
            scores = scores + bias
            old_max = both(max_ref)
            far_max = jnp.concatenate(
                [
                    jnp.broadcast_to(
                        jnp.max(scores[:, head(i)], axis=1, keepdims=True), (STACK * rows, HD)
                    )
                    for i in range(2)
                ],
                axis=1,
            )
            new_max = jnp.maximum(old_max, far_max)
            weights = jnp.exp2((scores - new_max) * exp2_scale)
            fade = jnp.exp2((old_max - new_max) * exp2_scale)
            far_sum = jnp.concatenate(
                [
                    jnp.broadcast_to(
                        jnp.sum(weights[:, head(i)], axis=1, keepdims=True), (STACK * rows, HD)
                    )
                    for i in range(2)
                ],
                axis=1,
            )
            mixed = jnp.dot(weights.astype(BF16), values, preferred_element_type=F32)
            total = both(sum_ref) * fade + far_sum
            mixed = ((both(mixed_ref) * fade + mixed) / total).astype(staged_ref.dtype)
            for side, columns in enumerate((left, right)):
                for i, at in enumerate(columns):
                    staged_ref[:, at] = mixed[i * rows : (i + 1) * rows, head(side)]
                at = slice(columns[0].start, columns[-1].stop)
                copy = pltpu.make_async_copy(
                    staged_ref.at[:, at], out_ref.at[:, at], sems.at[len(copies)]
                )
                copy.start()
                copies.append(copy)
    for copy in copies:
        copy.wait()


def on_chip(array):
    return pltpu.with_memory_space_constraint(array, pltpu.VMEM)


def attend(queries, near_keys, near_values, far_keys, far_values, relayed, seq_lengths):
    rows, width = queries.shape
    chunks = len(near_keys)
    shared = far_keys.shape[1] // HD
    group = width // far_keys.shape[1]
    whole = pl.BlockSpec(memory_space=pltpu.VMEM)
    params = pltpu.CompilerParams(vmem_limit_bytes=VMEM_LIMIT)
    queries = on_chip(queries)
    state = pltpu.VMEM((rows, width), F32)
    pairs = rows * width * chunks * rows
    row_max, row_sum, mixed, far_bias = pl.pallas_call(
        functools.partial(near_kernel, chunks, group),
        in_specs=[pl.BlockSpec(memory_space=pltpu.SMEM)] + [whole] * (1 + 2 * chunks),
        out_specs=[whole] * 4,
        out_shape=[state, state, state, pltpu.VMEM((rows, rows), F32)],
        scratch_shapes=[pltpu.VMEM((chunks * rows, 2 * HD), BF16)],
        compiler_params=params,
        cost_estimate=pl.CostEstimate(
            flops=6 * pairs, transcendentals=pairs // HD, bytes_accessed=rows * width * 14
        ),
        name="near",
    )(seq_lengths, queries, *map(on_chip, near_keys), *map(on_chip, near_values))
    copies = 2 * (shared // 2) * (group // STACK)
    return pl.pallas_call(
        functools.partial(far_kernel, group),
        in_specs=[whole] * 8,
        out_specs=pl.BlockSpec(memory_space=pl.ANY),
        out_shape=jax.ShapeDtypeStruct((rows, width), queries.dtype),
        scratch_shapes=[
            pltpu.VMEM(far_keys.shape, BF16),
            pltpu.VMEM((2 * rows, 2 * HD), BF16),
            pltpu.VMEM((2 * rows, 2 * HD), BF16),
            pltpu.VMEM((rows, width), queries.dtype),
            pltpu.SemaphoreType.DMA((copies,)),
        ],
        compiler_params=params,
        name="far",
    )(queries, on_chip(far_keys), on_chip(far_values), on_chip(relayed), far_bias, row_max, row_sum, mixed)


def body(queries, key_proj, value_proj, seq_lengths):
    rows = queries.shape[0]
    reach = rows * lax.axis_size("seq") // 2
    behind = -(-reach // rows)
    near_keys, near_values = [key_proj], [value_proj]
    for distance in range(1, behind):
        near_keys.insert(0, shift(key_proj, distance))
        near_values.insert(0, shift(value_proj, distance))
    far_keys = shift(key_proj, behind)
    far_values = shift(value_proj, behind, lambda target: target % 2 == 0)
    relayed = shift(near_values[0], 1, lambda target: target % 2 == 1 and target >= behind)
    return attend(queries, near_keys, near_values, far_keys, far_values, relayed, seq_lengths)


def solution(mesh):
    return jax.shard_map(
        body,
        mesh=mesh,
        in_specs=(P(AXES, None), P(AXES, None), P(AXES, None), P()),
        out_specs=P(AXES, None),
        check_vma=False,
    )
```

```python
import functools
import math

import jax
import jax.numpy as jnp
from jax import lax
from jax.experimental import pallas as pl
from jax.experimental.pallas import tpu as pltpu
from jax.sharding import PartitionSpec as P

HD = 128
STACK = 4
VMEM_LIMIT = 24 << 20

AXES = ("dp", "seq")
score_scale = 0.08838834764831845
neg_fill = -1e30
exp2_scale = score_scale * math.log2(math.e)

F32 = jnp.float32
BF16 = jnp.bfloat16


def shift(block, distance, keep=lambda target: True):
    count = lax.axis_size(AXES)
    return lax.ppermute(
        block, AXES, [(t - distance, t) for t in range(distance, count) if keep(t)]
    )


def head(index, count=1):
    return slice(index * HD, (index + count) * HD)


def row_stack(ref, columns):
    return jnp.concatenate([ref[:, at] for at in columns], axis=0)


def mask_bias(lengths_ref, rows, span):
    first = lax.axis_index(AXES) * rows
    key_pos = lax.broadcasted_iota(jnp.int32, (8, span), 1) + (first - span + rows)

    def step(i, carry):
        end, last = carry
        end = end + lengths_ref[i]
        return end, jnp.where(key_pos < end, jnp.minimum(last, end - 1), last)

    top = jnp.full((8, span), jnp.iinfo(jnp.int32).max, jnp.int32)
    _, last = lax.fori_loop(0, lengths_ref.shape[0], step, (jnp.int32(0), top), unroll=4)
    last = jnp.where(key_pos < 0, -1, last)
    query_pos = lax.broadcasted_iota(jnp.int32, (rows, span), 0) + first
    allowed = (query_pos >= key_pos[:1]) & (query_pos <= last[:1])
    return jnp.where(allowed, 0.0, neg_fill)


def near_kernel(chunks, group, lengths_ref, q_hbm, key_hbm, value_hbm, *refs):
    key_refs = refs[: chunks - 1]
    value_refs = refs[chunks - 1 : 2 * chunks - 2]
    q_ref, max_ref, sum_ref, mixed_ref, far_bias_ref, own_key, own_value, value_ref, sems = refs[
        2 * chunks - 2 :
    ]
    rows = q_ref.shape[0]
    span = chunks * rows
    shared = own_key.shape[1] // HD
    loads = [
        pltpu.make_async_copy(key_hbm, own_key, sems.at[0]),
        pltpu.make_async_copy(value_hbm, own_value, sems.at[1]),
    ]
    for kv in range(shared):
        at = head(kv * group, group)
        loads.append(pltpu.make_async_copy(q_hbm.at[:, at], q_ref.at[:, at], sems.at[2 + kv]))
    for load in loads:
        load.start()
    bias = mask_bias(lengths_ref, rows, span + rows)
    far_bias_ref[...] = bias[:, :rows]
    bias = jnp.concatenate([bias[:, rows:]] * STACK, axis=0)
    value_ref[:, HD:] = jnp.ones((span, HD), value_ref.dtype)
    loads[0].wait()
    loads[1].wait()
    for kv in range(shared):
        keys = jnp.concatenate([ref[:, head(kv)] for ref in (*key_refs, own_key)], axis=0)
        for i, ref in enumerate((*value_refs, own_value)):
            value_ref[i * rows : (i + 1) * rows, :HD] = ref[:, head(kv)]
        values = value_ref[...]
        loads[2 + kv].wait()
        for first in range(kv * group, (kv + 1) * group, STACK):
            columns = [head(first + i) for i in range(STACK)]
            scores = lax.dot_general(
                row_stack(q_ref, columns),
                keys,
                (((1,), (1,)), ((), ())),
                preferred_element_type=F32,
            )
            scores = scores + bias
            row_max = jnp.max(scores, axis=1, keepdims=True)
            weights = jnp.exp2((scores - row_max) * exp2_scale).astype(BF16)
            mixed = jnp.dot(weights, values, preferred_element_type=F32)
            row_max = jnp.broadcast_to(row_max, (STACK * rows, HD))
            for i, at in enumerate(columns):
                part = slice(i * rows, (i + 1) * rows)
                max_ref[:, at] = row_max[part]
                mixed_ref[:, at] = mixed[part, :HD]
                sum_ref[:, at] = mixed[part, HD:]


def block_diagonal(first, second, scratch):
    rows = first.shape[0]
    scratch[:rows, :HD] = first
    scratch[rows:, HD:] = second
    scratch[:rows, HD:] = jnp.zeros((rows, HD), scratch.dtype)
    scratch[rows:, :HD] = jnp.zeros((rows, HD), scratch.dtype)
    return scratch[...]


def head_pairs(shared, group):
    for a in range(0, shared, 2):
        for first in range(0, group, STACK):
            yield a, [
                [head((a + side) * group + first + i) for i in range(STACK)] for side in range(2)
            ]


def side_by_side(ref, columns):
    return jnp.concatenate([row_stack(ref, side) for side in columns], axis=1)


def put_pair(ref, columns, block):
    rows = ref.shape[0]
    for side in range(2):
        for i, at in enumerate(columns[side]):
            ref[:, at] = block[i * rows : (i + 1) * rows, head(side)]


def per_side(reduce, block):
    parts = [reduce(block[:, head(side)], axis=1, keepdims=True) for side in range(2)]
    return jnp.concatenate([jnp.broadcast_to(p, (block.shape[0], HD)) for p in parts], axis=1)


def far_kernel(group, q_ref, key_ref, bias_ref, max_ref, sum_ref, mixed_ref, weight_ref, scale_ref, faded_ref, pair_ref):
    shared = key_ref.shape[1] // HD
    bias = jnp.concatenate([bias_ref[...]] * STACK, axis=0)
    bias = jnp.concatenate([bias] * 2, axis=1)
    done = None
    for a, columns in head_pairs(shared, group):
        if a != done:
            keys = block_diagonal(key_ref[:, head(a)], key_ref[:, head(a + 1)], pair_ref)
            done = a
        scores = lax.dot_general(
            side_by_side(q_ref, columns), keys, (((1,), (1,)), ((), ())), preferred_element_type=F32
        )
        scores = scores + bias
        old_max = side_by_side(max_ref, columns)
        new_max = jnp.maximum(old_max, per_side(jnp.max, scores))
        weights = jnp.exp2((scores - new_max) * exp2_scale)
        fade = jnp.exp2((old_max - new_max) * exp2_scale)
        scale = 1.0 / (side_by_side(sum_ref, columns) * fade + per_side(jnp.sum, weights))
        put_pair(weight_ref, columns, weights.astype(BF16))
        put_pair(scale_ref, columns, scale)
        put_pair(faded_ref, columns, side_by_side(mixed_ref, columns) * (fade * scale))


def last_kernel(group, value_ref, relay_ref, weight_ref, scale_ref, faded_ref, out_ref, pair_ref, staged_ref, sems):
    shared = value_ref.shape[1] // HD
    copies = []
    done = None
    for a, columns in head_pairs(shared, group):
        if a != done:
            values = block_diagonal(
                *[value_ref[:, head(kv)] + relay_ref[:, head(kv)] for kv in (a, a + 1)], pair_ref
            )
            done = a
        mixed = jnp.dot(side_by_side(weight_ref, columns), values, preferred_element_type=F32)
        mixed = side_by_side(faded_ref, columns) + mixed * side_by_side(scale_ref, columns)
        put_pair(staged_ref, columns, mixed.astype(staged_ref.dtype))
        for side in columns:
            at = slice(side[0].start, side[-1].stop)
            copies.append(
                pltpu.make_async_copy(
                    staged_ref.at[:, at], out_ref.at[:, at], sems.at[len(copies)]
                )
            )
            copies[-1].start()
    for copy in copies:
        copy.wait()


def on_chip(array):
    return pltpu.with_memory_space_constraint(array, pltpu.VMEM)


def off_chip(array):
    return pltpu.with_memory_space_constraint(array, pltpu.HBM)


def attend(queries, near_keys, near_values, far_keys, far_values, relayed, seq_lengths):
    rows, width = queries.shape
    chunks = len(near_keys)
    shared = far_keys.shape[1] // HD
    group = width // far_keys.shape[1]
    whole = pl.BlockSpec(memory_space=pltpu.VMEM)
    outside = pl.BlockSpec(memory_space=pltpu.HBM)
    params = pltpu.CompilerParams(vmem_limit_bytes=VMEM_LIMIT)
    wide = pltpu.VMEM((rows, width), F32)
    narrow = pltpu.VMEM((rows, width), BF16)
    own = pltpu.VMEM(far_keys.shape, BF16)
    pair = pltpu.VMEM((2 * rows, 2 * HD), BF16)
    pairs = rows * width * rows
    *near_keys, own_keys = near_keys
    *near_values, own_values = near_values
    queries, row_max, row_sum, mixed, far_bias = pl.pallas_call(
        functools.partial(near_kernel, chunks, group),
        in_specs=[pl.BlockSpec(memory_space=pltpu.SMEM)] + [outside] * 3 + [whole] * (2 * chunks - 2),
        out_specs=[whole] * 5,
        out_shape=[narrow, wide, wide, wide, pltpu.VMEM((rows, rows), F32)],
        scratch_shapes=[
            own,
            own,
            pltpu.VMEM((chunks * rows, 2 * HD), BF16),
            pltpu.SemaphoreType.DMA((2 + shared,)),
        ],
        compiler_params=params,
        cost_estimate=pl.CostEstimate(
            flops=6 * chunks * pairs, transcendentals=chunks * pairs // HD, bytes_accessed=rows * width * 14
        ),
        name="near",
    )(
        *map(off_chip, (seq_lengths, queries, own_keys, own_values)),
        *map(on_chip, near_keys),
        *map(on_chip, near_values),
    )
    weights, scale, faded = pl.pallas_call(
        functools.partial(far_kernel, group),
        in_specs=[whole] * 6,
        out_specs=[whole] * 3,
        out_shape=[narrow, wide, wide],
        scratch_shapes=[pair],
        compiler_params=params,
        cost_estimate=pl.CostEstimate(
            flops=2 * pairs, transcendentals=pairs // HD, bytes_accessed=rows * width * 24
        ),
        name="far",
    )(queries, on_chip(far_keys), far_bias, row_max, row_sum, mixed)
    copies = 2 * (shared // 2) * (group // STACK)
    return pl.pallas_call(
        functools.partial(last_kernel, group),
        in_specs=[whole] * 5,
        out_specs=outside,
        out_shape=jax.ShapeDtypeStruct((rows, width), queries.dtype),
        scratch_shapes=[pair, narrow, pltpu.SemaphoreType.DMA((copies,))],
        compiler_params=params,
        name="last",
    )(on_chip(far_values), on_chip(relayed), weights, scale, faded)


def body(queries, key_proj, value_proj, seq_lengths):
    rows = queries.shape[0]
    reach = rows * lax.axis_size("seq") // 2
    behind = -(-reach // rows)
    near_keys, near_values = [key_proj], [value_proj]
    for distance in range(1, behind):
        near_keys.insert(0, shift(key_proj, distance))
        near_values.insert(0, shift(value_proj, distance))
    far_keys = shift(key_proj, behind)
    far_values = shift(value_proj, behind, lambda target: target % 2 == 0)
    relayed = shift(near_values[0], 1, lambda target: target % 2 == 1 and target >= behind)
    return attend(queries, near_keys, near_values, far_keys, far_values, relayed, seq_lengths)


def solution(mesh):
    return jax.shard_map(
        body,
        mesh=mesh,
        in_specs=(P(AXES, None), P(AXES, None), P(AXES, None), P()),
        out_specs=P(AXES, None),
        check_vma=False,
    )
```

```python
import functools
import math

import jax
import jax.numpy as jnp
from jax import lax
from jax.experimental import pallas as pl
from jax.experimental.pallas import tpu as pltpu
from jax.sharding import PartitionSpec as P

HD = 128
NEAR_STACK = 2
FAR_STACK = 2
LAST_STACK = 2
PIECE = 4
VMEM_LIMIT = 24 << 20

AXES = ("dp", "seq")
score_scale = 0.08838834764831845
neg_fill = -1e30
exp2_scale = score_scale * math.log2(math.e)

F32 = jnp.float32
BF16 = jnp.bfloat16


def shift(block, distance, keep=lambda target: True):
    count = lax.axis_size(AXES)
    return lax.ppermute(
        block, AXES, [(t - distance, t) for t in range(distance, count) if keep(t)]
    )


def head(index, count=1):
    return slice(index * HD, (index + count) * HD)


def row_stack(ref, columns):
    return jnp.concatenate([ref[:, at] for at in columns], axis=0)


def mask_bias(lengths_ref, rows, span):
    first = lax.axis_index(AXES) * rows
    key_pos = lax.broadcasted_iota(jnp.int32, (8, span), 1) + (first - span + rows)

    def step(i, carry):
        end, last = carry
        end = end + lengths_ref[i]
        return end, jnp.where(key_pos < end, jnp.minimum(last, end - 1), last)

    top = jnp.full((8, span), jnp.iinfo(jnp.int32).max, jnp.int32)
    _, last = lax.fori_loop(0, lengths_ref.shape[0], step, (jnp.int32(0), top), unroll=4)
    last = jnp.where(key_pos < 0, -1, last)
    query_pos = lax.broadcasted_iota(jnp.int32, (rows, span), 0) + first
    allowed = (query_pos >= key_pos[:1]) & (query_pos <= last[:1])
    return jnp.where(allowed, 0.0, neg_fill)


def near_kernel(chunks, group, lengths_hbm, q_hbm, key_hbm, value_hbm, *refs):
    key_refs = refs[: chunks - 1]
    value_refs = refs[chunks - 1 : 2 * chunks - 2]
    (
        q_ref,
        max_ref,
        sum_ref,
        mixed_ref,
        far_bias_ref,
        lengths_ref,
        own_key,
        own_value,
        value_ref,
        sems,
    ) = refs[2 * chunks - 2 :]
    rows = q_ref.shape[0]
    span = chunks * rows
    shared = own_key.shape[1] // HD
    loads = [
        pltpu.make_async_copy(lengths_hbm, lengths_ref, sems.at[0]),
        pltpu.make_async_copy(key_hbm, own_key, sems.at[1]),
        pltpu.make_async_copy(value_hbm, own_value, sems.at[2]),
    ]
    for kv in range(shared):
        at = head(kv * group, group)
        loads.append(pltpu.make_async_copy(q_hbm.at[:, at], q_ref.at[:, at], sems.at[3 + kv]))
    for load in loads:
        load.start()
    value_ref[:, HD:] = jnp.ones((span, HD), value_ref.dtype)
    loads[0].wait()
    bias = mask_bias(lengths_ref, rows, span + rows)
    far_bias_ref[...] = bias[:, :rows]
    bias = jnp.concatenate([bias[:, rows:]] * NEAR_STACK, axis=0)
    loads[1].wait()
    loads[2].wait()
    for kv in range(shared):
        keys = jnp.concatenate([ref[:, head(kv)] for ref in (*key_refs, own_key)], axis=0)
        for i, ref in enumerate((*value_refs, own_value)):
            value_ref[i * rows : (i + 1) * rows, :HD] = ref[:, head(kv)]
        values = value_ref[...]
        loads[3 + kv].wait()
        for first in range(kv * group, (kv + 1) * group, NEAR_STACK):
            columns = [head(first + i) for i in range(NEAR_STACK)]
            scores = lax.dot_general(
                row_stack(q_ref, columns),
                keys,
                (((1,), (1,)), ((), ())),
                preferred_element_type=F32,
            )
            scores = scores + bias
            row_max = jnp.max(scores, axis=1, keepdims=True)
            weights = jnp.exp2((scores - row_max) * exp2_scale).astype(BF16)
            mixed = jnp.dot(weights, values, preferred_element_type=F32)
            row_max = jnp.broadcast_to(row_max, (NEAR_STACK * rows, HD))
            for i, at in enumerate(columns):
                part = slice(i * rows, (i + 1) * rows)
                max_ref[:, at] = row_max[part]
                mixed_ref[:, at] = mixed[part, :HD]
                sum_ref[:, at] = mixed[part, HD:]


def block_diagonal(first, second, scratch):
    rows = first.shape[0]
    scratch[:rows, :HD] = first
    scratch[rows:, HD:] = second
    scratch[:rows, HD:] = jnp.zeros((rows, HD), scratch.dtype)
    scratch[rows:, :HD] = jnp.zeros((rows, HD), scratch.dtype)
    return scratch[...]


def head_pairs(shared, group, stack):
    for a in range(0, shared, 2):
        for first in range(0, group, stack):
            yield a, first, [
                [head((a + side) * group + first + i) for i in range(stack)] for side in range(2)
            ]


def side_by_side(ref, columns):
    return jnp.concatenate([row_stack(ref, side) for side in columns], axis=1)


def put_pair(ref, columns, block):
    rows = ref.shape[0]
    for side in range(2):
        for i, at in enumerate(columns[side]):
            ref[:, at] = block[i * rows : (i + 1) * rows, head(side)]


def per_side(reduce, block):
    parts = [reduce(block[:, head(side)], axis=1, keepdims=True) for side in range(2)]
    return jnp.concatenate([jnp.broadcast_to(p, (block.shape[0], HD)) for p in parts], axis=1)


def far_kernel(group, q_ref, key_ref, bias_ref, max_ref, sum_ref, mixed_ref, weight_ref, total_ref, faded_ref, pair_ref):
    shared = key_ref.shape[1] // HD
    bias = jnp.concatenate([bias_ref[...]] * FAR_STACK, axis=0)
    bias = jnp.concatenate([bias] * 2, axis=1)
    done = None
    for a, _, columns in head_pairs(shared, group, FAR_STACK):
        if a != done:
            keys = block_diagonal(key_ref[:, head(a)], key_ref[:, head(a + 1)], pair_ref)
            done = a
        scores = lax.dot_general(
            side_by_side(q_ref, columns), keys, (((1,), (1,)), ((), ())), preferred_element_type=F32
        )
        scores = scores + bias
        old_max = side_by_side(max_ref, columns)
        new_max = jnp.maximum(old_max, per_side(jnp.max, scores))
        weights = jnp.exp2((scores - new_max) * exp2_scale)
        fade = jnp.exp2((old_max - new_max) * exp2_scale)
        total = side_by_side(sum_ref, columns) * fade + per_side(jnp.sum, weights)
        put_pair(weight_ref, columns, weights.astype(BF16))
        put_pair(total_ref, columns, total)
        put_pair(faded_ref, columns, side_by_side(mixed_ref, columns) * fade)


def last_kernel(group, value_ref, relay_ref, weight_ref, total_ref, faded_ref, out_ref, pair_ref, staged_ref, sems):
    shared = value_ref.shape[1] // HD
    copies = []
    done = None
    for a, first, columns in head_pairs(shared, group, LAST_STACK):
        if a != done:
            values = block_diagonal(
                *[value_ref[:, head(kv)] + relay_ref[:, head(kv)] for kv in (a, a + 1)], pair_ref
            )
            done = a
        mixed = jnp.dot(side_by_side(weight_ref, columns), values, preferred_element_type=F32)
        mixed = (side_by_side(faded_ref, columns) + mixed) / side_by_side(total_ref, columns)
        put_pair(staged_ref, columns, mixed.astype(staged_ref.dtype))
        ready = first + LAST_STACK
        if ready % PIECE:
            continue
        for kv in (a, a + 1):
            at = head(kv * group + ready - PIECE, PIECE)
            copies.append(
                pltpu.make_async_copy(
                    staged_ref.at[:, at], out_ref.at[:, at], sems.at[len(copies)]
                )
            )
            copies[-1].start()
    for copy in copies:
        copy.wait()


def on_chip(array):
    return pltpu.with_memory_space_constraint(array, pltpu.VMEM)


def off_chip(array):
    return pltpu.with_memory_space_constraint(array, pltpu.HBM)


def attend(queries, near_keys, near_values, far_keys, far_values, relayed, seq_lengths):
    rows, width = queries.shape
    chunks = len(near_keys)
    shared = far_keys.shape[1] // HD
    group = width // far_keys.shape[1]
    whole = pl.BlockSpec(memory_space=pltpu.VMEM)
    outside = pl.BlockSpec(memory_space=pltpu.HBM)
    params = pltpu.CompilerParams(vmem_limit_bytes=VMEM_LIMIT)
    wide = pltpu.VMEM((rows, width), F32)
    narrow = pltpu.VMEM((rows, width), BF16)
    own = pltpu.VMEM(far_keys.shape, BF16)
    pair = pltpu.VMEM((2 * rows, 2 * HD), BF16)
    pairs = rows * width * rows
    *near_keys, own_keys = near_keys
    *near_values, own_values = near_values
    queries, row_max, row_sum, mixed, far_bias = pl.pallas_call(
        functools.partial(near_kernel, chunks, group),
        in_specs=[outside] * 4 + [whole] * (2 * chunks - 2),
        out_specs=[whole] * 5,
        out_shape=[narrow, wide, wide, wide, pltpu.VMEM((rows, rows), F32)],
        scratch_shapes=[
            pltpu.SMEM(seq_lengths.shape, seq_lengths.dtype),
            own,
            own,
            pltpu.VMEM((chunks * rows, 2 * HD), BF16),
            pltpu.SemaphoreType.DMA((3 + shared,)),
        ],
        compiler_params=params,
        cost_estimate=pl.CostEstimate(
            flops=6 * chunks * pairs, transcendentals=chunks * pairs // HD, bytes_accessed=rows * width * 14
        ),
        name="near",
    )(
        *map(off_chip, (seq_lengths, queries, own_keys, own_values)),
        *map(on_chip, near_keys),
        *map(on_chip, near_values),
    )
    weights, total, faded = pl.pallas_call(
        functools.partial(far_kernel, group),
        in_specs=[whole] * 6,
        out_specs=[whole] * 3,
        out_shape=[narrow, wide, wide],
        scratch_shapes=[pair],
        compiler_params=params,
        cost_estimate=pl.CostEstimate(
            flops=2 * pairs, transcendentals=pairs // HD, bytes_accessed=rows * width * 24
        ),
        name="far",
    )(queries, on_chip(far_keys), far_bias, row_max, row_sum, mixed)
    copies = shared * (group // PIECE)
    return pl.pallas_call(
        functools.partial(last_kernel, group),
        in_specs=[whole] * 5,
        out_specs=outside,
        out_shape=jax.ShapeDtypeStruct((rows, width), queries.dtype),
        scratch_shapes=[pair, narrow, pltpu.SemaphoreType.DMA((copies,))],
        compiler_params=params,
        name="last",
    )(on_chip(far_values), on_chip(relayed), weights, total, faded)


def body(queries, key_proj, value_proj, seq_lengths):
    rows = queries.shape[0]
    reach = rows * lax.axis_size("seq") // 2
    behind = -(-reach // rows)
    near_keys, near_values = [key_proj], [value_proj]
    for distance in range(1, behind):
        near_keys.insert(0, shift(key_proj, distance))
        near_values.insert(0, shift(value_proj, distance))
    far_keys = shift(key_proj, behind)
    far_values = shift(value_proj, behind, lambda target: target % 2 == 0)
    relayed = shift(near_values[0], 1, lambda target: target % 2 == 1 and target >= behind)
    return attend(queries, near_keys, near_values, far_keys, far_values, relayed, seq_lengths)


def solution(mesh):
    return jax.shard_map(
        body,
        mesh=mesh,
        in_specs=(P(AXES, None), P(AXES, None), P(AXES, None), P()),
        out_specs=P(AXES, None),
        check_vma=False,
    )
```

```python
import functools
import math

import jax
import jax.numpy as jnp
from jax import lax
from jax.experimental import pallas as pl
from jax.experimental.pallas import tpu as pltpu
from jax.sharding import PartitionSpec as P


HD = 128
NEAR_STACK = 2
FAR_STACK = 2
LAST_STACK = 2
PIECE = 8
EARLY_MEMBERS = lambda members: members // 2
PARTS = 1
VMEM_LIMIT = 24 << 20

AXES = ("dp", "seq")
score_scale = 0.08838834764831845
neg_fill = -1e30
exp2_scale = score_scale * math.log2(math.e)

F32 = jnp.float32
BF16 = jnp.bfloat16


def shift(block, distance, keep=lambda target: True):
    count = lax.axis_size(AXES)
    return lax.ppermute(block, AXES, [(t - distance, t) for t in range(distance, count) if keep(t)])


def head(index, count=1):
    return slice(index * HD, (index + count) * HD)


def row_stack(ref, columns):
    return jnp.concatenate([ref[:, at] for at in columns], axis=0)


def mask_bias(lengths_ref, rows, span):
    first = lax.axis_index(AXES) * rows
    key_pos = lax.broadcasted_iota(jnp.int32, (8, span), 1) + (first - span + rows)

    def step(i, carry):
        end, last = carry
        end = end + lengths_ref[i]
        return end, jnp.where(key_pos < end, jnp.minimum(last, end - 1), last)

    top = jnp.full((8, span), jnp.iinfo(jnp.int32).max, jnp.int32)
    _, last = lax.fori_loop(0, lengths_ref.shape[0], step, (jnp.int32(0), top), unroll=4)
    last = jnp.where(key_pos < 0, -1, last)
    query_pos = lax.broadcasted_iota(jnp.int32, (rows, span), 0) + first
    allowed = (query_pos >= key_pos[:1]) & (query_pos <= last[:1])
    return jnp.where(allowed, 0.0, neg_fill)


def load_kernel(early, lengths_hbm, q_hbm, key_hbm, value_hbm, *refs):
    is_early = lax.axis_index("seq") < EARLY_MEMBERS(lax.axis_size("seq"))
    pl.when(is_early if early else jnp.logical_not(is_early))(
        functools.partial(load_now, lengths_hbm, q_hbm, key_hbm, value_hbm, *refs[-7:])
    )


def load_now(lengths_hbm, q_hbm, key_hbm, value_hbm, *refs):
    q_ref, key_ref, value_ref, far_bias_ref, near_bias_ref, lengths_ref, sems = refs
    rows = q_ref.shape[0]
    span = near_bias_ref.shape[1]
    loads = [
        pltpu.make_async_copy(source, target, sems.at[i])
        for i, (source, target) in enumerate(
            (
                (lengths_hbm, lengths_ref),
                (q_hbm, q_ref),
                (key_hbm, key_ref),
                (value_hbm, value_ref),
            )
        )
    ]
    for load in loads:
        load.start()
    loads[0].wait()
    bias = mask_bias(lengths_ref, rows, span + rows)
    far_bias_ref[...] = bias[:, :rows]
    near_bias_ref[...] = bias[:, rows:]
    for load in loads[1:]:
        load.wait()


def near_kernel(chunks, group, q_ref, bias_ref, *refs):
    key_refs = refs[:chunks]
    value_refs = refs[chunks : 2 * chunks]
    max_ref, sum_ref, mixed_ref, value_ref = refs[2 * chunks :]
    rows = q_ref.shape[0]
    shared = key_refs[0].shape[1] // HD
    value_ref[:, HD:] = jnp.ones((chunks * rows, HD), value_ref.dtype)
    bias = jnp.concatenate([bias_ref[...]] * NEAR_STACK, axis=0)
    for kv in range(shared):
        keys = jnp.concatenate([ref[:, head(kv)] for ref in key_refs], axis=0)
        for i, ref in enumerate(value_refs):
            value_ref[i * rows : (i + 1) * rows, :HD] = ref[:, head(kv)]
        values = value_ref[...]
        for first in range(kv * group, (kv + 1) * group, NEAR_STACK):
            columns = [head(first + i) for i in range(NEAR_STACK)]
            scores = lax.dot_general(
                row_stack(q_ref, columns),
                keys,
                (((1,), (1,)), ((), ())),
                preferred_element_type=F32,
            )
            scores = scores + bias
            row_max = jnp.max(scores, axis=1, keepdims=True)
            weights = jnp.exp2((scores - row_max) * exp2_scale).astype(BF16)
            mixed = jnp.dot(weights, values, preferred_element_type=F32)
            row_max = jnp.broadcast_to(row_max, (NEAR_STACK * rows, HD))
            for i, at in enumerate(columns):
                part = slice(i * rows, (i + 1) * rows)
                max_ref[:, at] = row_max[part]
                mixed_ref[:, at] = mixed[part, :HD]
                sum_ref[:, at] = mixed[part, HD:]


def block_diagonal(first, second, scratch):
    rows = first.shape[0]
    scratch[:rows, :HD] = first
    scratch[rows:, HD:] = second
    scratch[:rows, HD:] = jnp.zeros((rows, HD), scratch.dtype)
    scratch[rows:, :HD] = jnp.zeros((rows, HD), scratch.dtype)
    return scratch[...]


def head_pairs(shared, group, stack):
    for a in range(0, shared, 2):
        for first in range(0, group, stack):
            yield a, first, [
                [head((a + side) * group + first + i) for i in range(stack)] for side in range(2)
            ]


def side_by_side(ref, part, columns):
    return jnp.concatenate(
        [jnp.concatenate([ref[part, at] for at in side], axis=0) for side in columns], axis=1
    )


def put_pair(ref, part, columns, block):
    rows = part.stop - part.start
    for side in range(2):
        for i, at in enumerate(columns[side]):
            ref[part, at] = block[i * rows : (i + 1) * rows, head(side)]


def per_side(reduce, block):
    parts = [reduce(block[:, head(side)], axis=1, keepdims=True) for side in range(2)]
    return jnp.concatenate([jnp.broadcast_to(p, (block.shape[0], HD)) for p in parts], axis=1)


def joined(refs, kv):
    return functools.reduce(jnp.add, [ref[:, head(kv)] for ref in refs])


def row_parts(bias_ref):
    size = bias_ref.shape[0] // PARTS
    for start in range(0, bias_ref.shape[0], size):
        yield slice(start, start + size), jnp.max(bias_ref[start : start + 8]) > neg_fill / 2


def far_kernel(pieces, group, *refs):
    key_refs = refs[:pieces]
    (
        q_ref,
        bias_ref,
        max_ref,
        sum_ref,
        mixed_ref,
        weight_ref,
        total_ref,
        faded_ref,
        pair_ref,
    ) = refs[pieces:]
    shared = key_refs[0].shape[1] // HD

    def merge(part):
        bias = jnp.concatenate([bias_ref[part]] * FAR_STACK, axis=0)
        bias = jnp.concatenate([bias] * 2, axis=1)
        for a, first, columns in head_pairs(shared, group, FAR_STACK):
            if first == 0:
                keys = block_diagonal(joined(key_refs, a), joined(key_refs, a + 1), pair_ref)
            scores = lax.dot_general(
                side_by_side(q_ref, part, columns),
                keys,
                (((1,), (1,)), ((), ())),
                preferred_element_type=F32,
            )
            scores = scores + bias
            old_max = side_by_side(max_ref, part, columns)
            new_max = jnp.maximum(old_max, per_side(jnp.max, scores))
            weights = jnp.exp2((scores - new_max) * exp2_scale)
            fade = jnp.exp2((old_max - new_max) * exp2_scale)
            total = side_by_side(sum_ref, part, columns) * fade + per_side(jnp.sum, weights)
            put_pair(weight_ref, part, columns, weights.astype(BF16))
            put_pair(total_ref, part, columns, total)
            put_pair(faded_ref, part, columns, side_by_side(mixed_ref, part, columns) * fade)

    for part, sees_far in row_parts(bias_ref):
        pl.when(sees_far)(functools.partial(merge, part))


def last_kernel(pieces, group, *refs):
    value_refs = refs[:pieces]
    (
        bias_ref,
        sum_ref,
        mixed_ref,
        weight_ref,
        total_ref,
        faded_ref,
        out_ref,
        pair_ref,
        staged_ref,
        sems,
    ) = refs[pieces:]
    shared = value_refs[0].shape[1] // HD
    parts = list(row_parts(bias_ref))

    def copy(index, part, kv, piece):
        at = head(kv * group + piece * PIECE, PIECE)
        number = (index * shared + kv) * (group // PIECE) + piece
        return pltpu.make_async_copy(
            staged_ref.at[part, at], out_ref.at[part, at], sems.at[number]
        )

    def finish(index, part, sees_far):
        for a, first, columns in head_pairs(shared, group, LAST_STACK):
            mixed = side_by_side(faded_ref if sees_far else mixed_ref, part, columns)
            if sees_far:
                if first == 0:
                    values = block_diagonal(
                        joined(value_refs, a), joined(value_refs, a + 1), pair_ref
                    )
                mixed = mixed + jnp.dot(
                    side_by_side(weight_ref, part, columns), values, preferred_element_type=F32
                )
            mixed = mixed / side_by_side(total_ref if sees_far else sum_ref, part, columns)
            put_pair(staged_ref, part, columns, mixed.astype(staged_ref.dtype))
            ready = first + LAST_STACK
            if ready % PIECE == 0:
                for kv in (a, a + 1):
                    copy(index, part, kv, ready // PIECE - 1).start()

    for index, (part, sees_far) in enumerate(parts):
        pl.when(sees_far)(functools.partial(finish, index, part, True))
        pl.when(jnp.logical_not(sees_far))(functools.partial(finish, index, part, False))
    for index, (part, _) in enumerate(parts):
        for kv in range(shared):
            for piece in range(group // PIECE):
                copy(index, part, kv, piece).wait()


def on_chip(array):
    return pltpu.with_memory_space_constraint(array, pltpu.VMEM)


def off_chip(array):
    return pltpu.with_memory_space_constraint(array, pltpu.HBM)


def attend(queries, near_keys, near_values, far_keys, far_values, seq_lengths):
    rows, width = queries.shape
    chunks = len(near_keys)
    shared = near_keys[0].shape[1] // HD
    group = width // near_keys[0].shape[1]
    whole = pl.BlockSpec(memory_space=pltpu.VMEM)
    outside = pl.BlockSpec(memory_space=pltpu.HBM)
    params = pltpu.CompilerParams(vmem_limit_bytes=VMEM_LIMIT)
    wide = pltpu.VMEM((rows, width), F32)
    narrow = pltpu.VMEM((rows, width), BF16)
    own = pltpu.VMEM(near_keys[0].shape, BF16)
    pair = pltpu.VMEM((2 * rows, 2 * HD), BF16)
    pairs = rows * width * rows
    *near_keys, own_keys = near_keys
    *near_values, own_values = near_values
    given = [off_chip(array) for array in (seq_lengths, queries, own_keys, own_values)]
    loaded = []
    for early in (True, False):
        loaded = pl.pallas_call(
            functools.partial(load_kernel, early),
            in_specs=[outside] * 4 + [whole] * len(loaded),
            out_specs=[whole] * 5,
            out_shape=[
                narrow,
                own,
                own,
                pltpu.VMEM((rows, rows), F32),
                pltpu.VMEM((rows, chunks * rows), F32),
            ],
            scratch_shapes=[
                pltpu.SMEM(seq_lengths.shape, seq_lengths.dtype),
                pltpu.SemaphoreType.DMA((4,)),
            ],
            input_output_aliases={4 + i: i for i in range(len(loaded))},
            compiler_params=params,
            name="early" if early else "load",
        )(*given, *loaded)
    queries, own_keys, own_values, far_bias, near_bias = loaded
    row_max, row_sum, mixed = pl.pallas_call(
        functools.partial(near_kernel, chunks, group),
        in_specs=[whole] * (2 + 2 * chunks),
        out_specs=[whole] * 3,
        out_shape=[wide, wide, wide],
        scratch_shapes=[pltpu.VMEM((chunks * rows, 2 * HD), BF16)],
        compiler_params=params,
        cost_estimate=pl.CostEstimate(
            flops=6 * chunks * pairs,
            transcendentals=chunks * pairs // HD,
            bytes_accessed=rows * width * 14,
        ),
        name="near",
    )(queries, near_bias, *map(on_chip, near_keys), own_keys, *map(on_chip, near_values), own_values)
    weights, total, faded = pl.pallas_call(
        functools.partial(far_kernel, len(far_keys), group),
        in_specs=[whole] * (5 + len(far_keys)),
        out_specs=[whole] * 3,
        out_shape=[narrow, wide, wide],
        scratch_shapes=[pair],
        compiler_params=params,
        cost_estimate=pl.CostEstimate(
            flops=2 * pairs, transcendentals=pairs // HD, bytes_accessed=rows * width * 24
        ),
        name="far",
    )(*map(on_chip, far_keys), queries, far_bias, row_max, row_sum, mixed)
    copies = PARTS * shared * (group // PIECE)
    return pl.pallas_call(
        functools.partial(last_kernel, len(far_values), group),
        in_specs=[whole] * (6 + len(far_values)),
        out_specs=outside,
        out_shape=jax.ShapeDtypeStruct((rows, width), queries.dtype),
        scratch_shapes=[pair, narrow, pltpu.SemaphoreType.DMA((copies,))],
        compiler_params=params,
        name="last",
    )(*map(on_chip, far_values), far_bias, row_sum, mixed, weights, total, faded)


def plan(rows, members):
    behind = -(-(rows * members // 2) // rows)
    return behind, lambda t: t % members < behind


def body(queries, key_proj, value_proj, seq_lengths):
    rows = queries.shape[0]
    members = lax.axis_size("seq")
    behind, _ = plan(rows, members)
    near_keys, near_values = [key_proj], [value_proj]
    for distance in range(1, behind):
        near_keys.insert(0, shift(key_proj, distance))
        near_values.insert(0, shift(value_proj, distance))
    far_keys = [
        shift(key_proj, behind, lambda t: t % members != 1),
        shift(near_keys[0], 1, lambda t: t % members == 1 and t >= behind),
    ]
    far_values = [
        shift(value_proj, behind, lambda t: t % members == 0),
        shift(near_values[0], 1, lambda t: t % members > 0 and t >= behind),
    ]
    return attend(queries, near_keys, near_values, far_keys, far_values, seq_lengths)


def solution(mesh):
    return jax.shard_map(
        body,
        mesh=mesh,
        in_specs=(P(AXES, None), P(AXES, None), P(AXES, None), P()),
        out_specs=P(AXES, None),
        check_vma=False,
    )
```
